128 devices in a mesh: gz: 8 (over x, core), xy: 16 (over y, z).
Axes of the slice: x: 4, y: 4, z: 4, core: 2. Of those that a mesh axis runs over, the one named last changes fastest.
Arguments:
- volume: bfloat16 [256, 64, 40960], P('gz', None, 'xy'), may hold values from -6 to 6
- occupancy: int32 [8, 320], P('gz', 'xy'), may hold values from 0 to 1, as said below
- device_order: int32 [8, 16], P('gz'), may hold values from 0 to 15, each once within a row
- weight_one: bfloat16 [64, 576], replicated, may hold values from -0.25 to 0.25
- bias_one: float32 [64], replicated, may hold values from -3 to 3
- weight_two: bfloat16 [64, 1728], replicated, may hold values from -0.15625 to 0.15625
- bias_two: float32 [64], replicated, may hold values from -3 to 3
Outputs:
- features: bfloat16 [1280, 64, 512], P(('gz', 'xy'))
The draws below stay inside these ranges and needn't reach their ends.
Inputs may be any that keep to these rules, and one draw needn't show every extreme that they name: `occupancy`: each slab holds exactly 160 tissue bricks, and in each slab all 20 bricks of one xy index are tissue. `device_order`: each slab's row names every xy index once.
All inputs are finite; a program needn't handle non-finite values.
Results may differ from the reference program's by a relative error of at most 0.0025.
Values may be sent and summed in bfloat16 or wider, within the bound.
No kernel may reach another device: no remote copies, remote signals or barrier semaphores. Data moves between devices by JAX's collectives and lax.ppermute only.
A program may use at most 256 MiB of HBM per device.

```python
import jax
import jax.numpy as jnp
from jax import lax

C = 64
BRICK = 32
XW = 4
COLS = 20
KC = 10
NZV = 256
NYX = 40960
N_GZ = 8
N_XY = 16


def draw_occupancy(key, part):
    slot_total = N_XY * COLS
    wanted_total = N_XY * KC

    def one_slab(slab_index):
        slab_key = jax.random.fold_in(jax.random.fold_in(key, 7121), slab_index)
        full_key, score_key, bias_key = jax.random.split(slab_key, 3)
        chosen = jax.random.randint(full_key, (), 0, N_XY)
        owner = jnp.arange(slot_total, dtype=jnp.int32) // COLS
        device_bias = jax.random.randint(bias_key, (N_XY,), 0, 4)
        noise = jax.random.randint(score_key, (slot_total,), 0, 4096)
        position = jnp.arange(slot_total, dtype=jnp.int32)
        score = (device_bias[owner] * 1024 + noise) * slot_total + position
        score = jnp.where(owner == chosen, 16384 * slot_total + position, score)
        ordering = jnp.argsort(-score, stable=True)
        placing = jnp.argsort(ordering, stable=True)
        return (placing < wanted_total).astype(jnp.int32)
    return jax.vmap(one_slab)(jnp.arange(N_GZ, dtype=jnp.int32))


def steps_of(key, extent, cuts, low, high):
    def one(dim, blocks):
        draws = jax.random.uniform(jax.random.fold_in(jax.random.fold_in(key, 6), dim), (blocks,), jnp.float32, low / len(cuts), high / len(cuts))
        return jnp.repeat(jnp.exp(draws), extent[dim] // blocks).reshape((-1,) + (1,) * (len(extent) - dim - 1))

    factor_of = one(*cuts[0])
    for cut in cuts[1:]:
        factor_of = factor_of * one(*cut)
    return factor_of


def gaussian(rng, dims, scale, limit, cuts=(), kind=jnp.bfloat16):
    array = jax.random.normal(rng, dims, jnp.float32) * scale
    if len(cuts) > 0:
        array = steps_of(rng, dims, cuts, -0.22, 0.18) * array
    return jnp.clip(array, min=-limit, max=limit).astype(kind)


def setup_inputs(seed: int = 0) -> dict:
    seeds = jax.random.split(jax.random.key(seed), 8)
    return {
        "volume": gaussian(seeds[0], (NZV, C, NYX), 1.0, 6.0, ((0, 8), (2, 16))),
        "occupancy": draw_occupancy(jax.random.fold_in(seeds[7], 71), 0),
        "device_order": jax.vmap(lambda own: jax.random.permutation(own, N_XY))(jax.random.split(seeds[2], N_GZ)).reshape((N_GZ, N_XY)).astype(jnp.int32),
        "weight_one": gaussian(seeds[3], (C, 9 * C), (9 * C) ** -0.5, 0.25),
        "bias_one": gaussian(seeds[4], (C,), 0.5, 3.0, (), jnp.float32),
        "weight_two": gaussian(seeds[5], (C, 27 * C), (27 * C) ** -0.5, 0.15625),
        "bias_two": gaussian(seeds[6], (C,), 0.5, 3.0, (), jnp.float32),
    }


def zone_table(length):
    position = jnp.arange(length)
    lower_end = (position == 0).astype(jnp.float32)
    upper_end = (position == length - 1).astype(jnp.float32)
    middle = 1.0 - lower_end - upper_end
    return jnp.stack([lower_end, middle, upper_end], axis=1)


def conv_chain(extended, flags, weight_one, bias_one, weight_two, bias_two):
    layers, channels, rows_ext, across = extended.shape
    inner_size = layers - 2
    moved_axes = jnp.transpose(extended, (1, 0, 2, 3))
    padded = jnp.pad(moved_axes, ((0, 0), (0, 0), (0, 0), (1, 1)))
    first_taps = [padded[:, :, row_tap:row_tap + inner_size + 2, col_tap:col_tap + across] for row_tap in range(3) for col_tap in range(3)]
    first_patches = jnp.concatenate(first_taps, axis=0).reshape(9 * channels, -1)
    first_sum = jnp.dot(weight_one, first_patches, preferred_element_type=jnp.float32)
    first_act = jax.nn.relu(first_sum + bias_one[:, None]).reshape(channels, layers, inner_size + 2, across)
    region = jnp.einsum("za,ab,yb->zy", zone_table(layers), flags.astype(jnp.float32), zone_table(inner_size + 2))
    hidden = (first_act * region[None, :, :, None]).astype(jnp.bfloat16)
    hidden_pad = jnp.pad(hidden, ((0, 0), (0, 0), (0, 0), (1, 1)))
    second_taps = [hidden_pad[:, :, row_tap:row_tap + inner_size, col_tap:col_tap + across] for row_tap in range(3) for col_tap in range(3)]
    second_patches = jnp.concatenate(second_taps, axis=0)
    second_sum = jnp.zeros((channels, inner_size * inner_size * across), jnp.float32)
    for layer_tap in range(3):
        section = second_patches[:, layer_tap:layer_tap + inner_size].reshape(9 * channels, -1)
        weights = weight_two[:, layer_tap * 9 * channels:(layer_tap + 1) * 9 * channels]
        second_sum = second_sum + jnp.dot(weights, section, preferred_element_type=jnp.float32)
    second_act = jax.nn.relu(second_sum + bias_two[:, None])
    second_act = second_act.reshape(channels, inner_size // 2, 2, inner_size // 2, 2, across // 2, 2)
    pooled = jnp.mean(second_act, axis=(2, 4, 6))
    return pooled.reshape(channels, -1).astype(jnp.bfloat16)


def neighbour_part(volume, occupancy, slab_index, column, shift_z, shift_y):
    slab_count = occupancy.shape[0]
    column_count = occupancy.shape[1]
    target_z = slab_index + shift_z
    target_y = column + shift_y
    inside = (target_z >= 0) & (target_z < slab_count) & (target_y >= 0) & (target_y < column_count)
    clip_z = jnp.clip(target_z, 0, slab_count - 1).astype(jnp.int32)
    clip_y = jnp.clip(target_y, 0, column_count - 1).astype(jnp.int32)
    present = jnp.where(inside, occupancy[clip_z, clip_y], 0)
    start_z = (clip_z * BRICK).astype(jnp.int32)
    start_y = (clip_y * (BRICK * XW)).astype(jnp.int32)
    block_data = lax.dynamic_slice(volume, (start_z, jnp.int32(0), start_y), (BRICK, C, BRICK * XW))
    block_data = block_data.reshape(BRICK, C, BRICK, XW)
    if shift_z == -1:
        block_data = block_data[BRICK - 1:]
    elif shift_z == 1:
        block_data = block_data[:1]
    if shift_y == -1:
        block_data = block_data[:, :, BRICK - 2:]
    elif shift_y == 1:
        block_data = block_data[:, :, :2]
    return block_data * present.astype(volume.dtype), present


def reference(volume, occupancy, device_order, weight_one, bias_one, weight_two, bias_two):
    ranked = jnp.argsort(1 - occupancy, axis=1, stable=True).astype(jnp.int32)
    inverse = jnp.argsort(device_order, axis=1).astype(jnp.int32)

    def one_slot(flat_index):
        slab_index = flat_index // (N_XY * KC)
        device = (flat_index // KC) % N_XY
        slot_index = flat_index % KC
        label_index = inverse[slab_index, device]
        column = ranked[slab_index, slot_index * N_XY + label_index]
        layer_rows = []
        flag_rows = []
        for shift_z in (-1, 0, 1):
            pieces = []
            marks = []
            for shift_y in (-1, 0, 1):
                piece_data, present = neighbour_part(volume, occupancy, slab_index, column, shift_z, shift_y)
                pieces.append(piece_data)
                marks.append(present.astype(jnp.float32))
            layer_rows.append(jnp.concatenate(pieces, axis=2))
            flag_rows.append(jnp.stack(marks))
        extended = jnp.concatenate(layer_rows, axis=0)
        flags = jnp.stack(flag_rows)
        return conv_chain(extended, flags, weight_one, bias_one, weight_two, bias_two)

    return lax.map(one_slot, jnp.arange(N_GZ * N_XY * KC, dtype=jnp.int32))
```

```python
import functools

import jax
import jax.numpy as jnp
from jax import lax
from jax.experimental import pallas as pl
from jax.experimental.pallas import tpu as pltpu
from jax.sharding import PartitionSpec as P

SEG = 16
HALF = 64


def shift(value, axis, step):
    peers = lax.axis_size(axis)
    pairs = [(i, i + step) for i in range(peers) if 0 <= i + step < peers]
    return lax.ppermute(value, axis, pairs)


EMPTY = 100.0
BREAKS = (-2, 0, 8, 16, 24, 32, 40, 42)


def span(t):
    return max(i for i, start in enumerate(BREAKS) if start <= t)


FRONT, PAD = 16, 4


class Spread:
    def __init__(self, work, steps):
        self.work, self.steps, self.done = list(work), steps, 0

    def step(self):
        self.done += 1
        for piece in self.work[
            len(self.work) * (self.done - 1) // self.steps:len(self.work) * self.done // self.steps
        ]:
            piece()


def mix(one, two):
    places = [((i + 0.5) / len(part), piece) for part in (one, two) for i, piece in enumerate(part)]
    return [piece for _, piece in sorted(places, key=lambda entry: entry[0])]


def features_kernel(
    order_ref, near_ref, far1_ref, far2_ref, far3_ref, first_ref, vol0_ref, vol1_ref, vol2_ref, vol3_ref, below_ref, above_ref,
    left_ref, right_ref, w1_ref, b1_ref, w2_ref, b2_ref,
    sent_ref, arrival_ref, flip, taps, hidden, masks, pooled, staged, slots, sems,
):
    group = pl.program_id(0)
    last = group == pl.num_programs(0) - 1
    chans, lanes = vol0_ref.shape[1], vol0_ref.shape[2]
    columns = lanes // 128
    runs = lanes // (4 * SEG)
    low = lax.broadcasted_iota(jnp.int32, (SEG, 128), 1) < HALF
    low8 = lax.broadcasted_iota(jnp.int32, (8, 128), 1) < HALF
    body_rows = runs * SEG
    first_rows = body_rows + 2 * SEG

    own = lax.axis_index("xy")
    groups = 4 * near_ref.shape[0]
    fars = (near_ref, far1_ref, far2_ref, far3_ref)

    def route():
        counts = []
        for k in range(groups):
            marks = fars[k // 4]
            count = marks[k % 4, 0]
            for j in range(1, columns):
                count = count + marks[k % 4, j]
            counts.append(count)
        start = jnp.int32(0)
        for k in range(1, groups):
            start = start + jnp.where((own ^ k) < own, counts[k], 0)
        rank = jnp.int32(0)
        for j in range(columns):
            full = near_ref[0, j]
            to = order_ref[0, (start + rank) & (groups - 1)]
            slots[j] = jnp.where(full > 0, 2 * to + (rank >= groups).astype(jnp.int32), -1)
            rank = rank + full
        label = jnp.int32(0)
        for i in range(groups):
            label = label + jnp.where(order_ref[0, i] == own, i, 0)
        for k in range(groups):
            begin = jnp.int32(0)
            for m in range(groups):
                if m != k:
                    begin = begin + jnp.where((own ^ m) < (own ^ k), counts[m], 0)
            ahead = (label - begin) & (groups - 1)
            for second in range(2):
                at = ahead + groups * second

                @pl.when(at < counts[k])
                def _():
                    arrival_ref[(begin + at) // groups] = 2 * (own ^ k) + second

    def turn_pieces(source, at_rim):
        def piece(j):
            block = jnp.concatenate([source(0, 128 * j), source(1, 128 * j)], axis=0)
            block = block.astype(jnp.float32).T
            start = 128 * j
            while start < 128 * j + 128:
                s = start // (4 * runs)
                stop = min(128 * j + 128, 4 * runs * (s + 1))
                to = FRONT + PAD * s + start
                flip[to:to + stop - start, :] = block[start - 128 * j:stop - 128 * j]
                start = stop

        def sides():
            flip[FRONT - PAD - 8:FRONT - PAD, :] = left_ref[at_rim].astype(jnp.float32)
            end = FRONT + SEG * (4 * runs + PAD)
            flip[end:end + 8, :] = right_ref[at_rim].astype(jnp.float32)

        return [sides] + [functools.partial(piece, j) for j in range(columns)]

    def turn(source, at_rim):
        for piece in turn_pieces(source, at_rim):
            piece()

    def row_tiles(t):
        start = FRONT + 4 * t + (-PAD if t < 0 else PAD if t >= runs else 0)
        rows = [flip[pl.ds(start + x, SEG, stride=4 * runs + PAD), :] for x in range(4)]
        turned = [pltpu.roll(row, HALF, 1) for row in rows]
        return [
            [
                jnp.where(low, rows[2 * h], turned[2 * h + 1]).astype(jnp.bfloat16)
                for h in range(2)
            ],
            [
                jnp.where(low, turned[2 * h], rows[2 * h + 1]).astype(jnp.bfloat16)
                for h in range(2)
            ],
        ]

    def store_taps(slot, layer, t, tiles, keep):
        for h in range(2):
            taps[slot, layer, SEG * (t + 2):SEG * (t + 3), 128 * h:128 * h + 128] = (
                tiles[layer][h] * keep
            )

    def row_pieces(slot, kinds):
        def piece(t):
            tiles = row_tiles(t)
            for layer in range(2):
                store_taps(slot, layer, t, tiles, masks[kinds[layer], span(t)])

        return [functools.partial(piece, t) for t in range(-2, runs + 2)]

    def first_dots(slot, work=()):
        total = None
        work = Spread(work, 3)
        for b in range(3):
            part = jnp.dot(
                taps[slot, :, SEG * b:SEG * b + first_rows, :].reshape(2 * first_rows, 256),
                w1_ref[b], preferred_element_type=jnp.float32,
            )
            total = part if total is None else total + part
            work.step()
        return total

    def first_pieces(total, kinds, places):
        def piece(layer, lo, hi, keep):
            at = layer * first_rows
            act = total[at + SEG * lo:at + SEG * hi]
            act = jnp.maximum(act + b1_ref[...], 0.0).astype(jnp.bfloat16)
            act = act.reshape(hi - lo, SEG, 256)
            for h in range(2):
                hidden[places[layer], SEG * lo:SEG * hi, 128 * h:128 * h + 128] = (
                    act[:, :, 128 * h:128 * h + 128] * keep()[None]
                ).reshape(SEG * (hi - lo), 128)

        made = []
        for layer in range(2):
            for i in range(len(BREAKS) - 1):
                lo, hi = max(BREAKS[i], -1) + 1, min(BREAKS[i + 1], runs + 1) + 1
                keep = functools.partial(lambda kind, i: masks[kind, i], kinds[layer], i)
                made.append(functools.partial(piece, layer, lo, hi, keep))
        return made

    def first_conv(slot, kinds, places):
        for piece in first_pieces(first_dots(slot), kinds, places):
            piece()

    def second_dots(places, ends, early, late):
        total = None
        early, late = Spread(early, 6), Spread(late, 9)
        for a in range(3):
            for b in range(3):
                rows = slice(SEG * b, SEG * b + body_rows)
                later = hidden[places[a + 1], rows, :]
                if ends and a == 2:
                    later = jnp.where(last, hidden[8, rows, :], later)
                part = jnp.dot(
                    jnp.concatenate([hidden[places[a], rows, :], later], axis=0),
                    w2_ref[3 * a + b], preferred_element_type=jnp.float32,
                )
                total = part if total is None else total + part
                if a < 2:
                    early.step()
                late.step()
        return total

    def second_pieces(slot, total):
        def piece(u):
            summed = None
            for at in (2 * u, 2 * u + 1, runs + 2 * u, runs + 2 * u + 1):
                part = jnp.maximum(total[SEG * at:SEG * at + SEG] + b2_ref[...], 0.0)
                summed = part if summed is None else summed + part
            for x2 in range(2):
                half = summed[:, 128 * x2:128 * x2 + 128]
                half = (half + pltpu.roll(half, HALF, 1)) * 0.125
                both = jnp.where(low8, half[0:8], half[8:16])
                pooled[slot, pl.ds(2 * u + x2, 8, stride=runs), :] = both

        return [functools.partial(piece, u) for u in range(runs // 2)]

    def of(ref):
        return lambda layer, at: ref[layer, :, at:at + 128]

    @pl.when(group == 0)
    def _():
        row = lax.broadcasted_iota(jnp.int32, (SEG, 128), 0)
        one, zero = jnp.ones((SEG, 128), jnp.bfloat16), jnp.zeros((SEG, 128), jnp.bfloat16)
        has = [
            lax.axis_index("gz") > 0, lax.axis_index("gz") < lax.axis_size("gz") - 1,
            own > 0, own < groups - 1,
        ]
        route()

        def inside(i):
            keep = None
            if BREAKS[i] < 0:
                keep = has[2] | (row > 0)
            elif BREAKS[i] >= runs:
                keep = has[3] | (row < SEG - 1)
            return keep

        turn(lambda layer, at: (below_ref, above_ref)[layer][0, :, at:at + 128], 0)
        for t in range(-2, runs + 2):
            tiles = row_tiles(t)
            for layer in range(2):
                i = span(t)
                if t == BREAKS[i]:
                    keep = (tiles[layer][0].astype(jnp.float32) < 50.0) & has[layer]
                    if inside(i) is not None:
                        keep = keep & inside(i)
                    masks[layer, i] = jnp.where(keep, 1.0, 0.0).astype(jnp.bfloat16)
                store_taps(0, layer, t, tiles, masks[layer, i])
        first_conv(0, [0, 1], [7, 8])

        turn(of(first_ref), 1)
        for i in range(len(BREAKS) - 1):
            t = BREAKS[i]
            keep = jnp.zeros((SEG, 128), jnp.float32)
            for s in range(SEG):
                column = (runs * s + t) // 32
                if 0 <= column < columns:
                    keep = jnp.where(row == s, near_ref[0, column].astype(jnp.float32), keep)
            keep = keep > 0.5
            seen = row_tiles(t)[0][0].astype(jnp.float32) < 50.0
            if t < 0:
                keep = keep | ((row == 0) & seen & has[2])
            elif t >= runs:
                keep = keep | ((row == SEG - 1) & seen & has[3])
            masks[2, i] = jnp.where(keep, 1.0, 0.0).astype(jnp.bfloat16)
        for t in range(-2, runs + 2):
            tiles = row_tiles(t)
            for layer in range(2):
                store_taps(0, layer, t, tiles, masks[2, span(t)])
        first_conv(0, [2, 2], [0, 1])
        turn(lambda layer, at: first_ref[2 + layer, :, at:at + 128], 2)
        for piece in row_pieces(1, [2, 2]):
            piece()

    top = left_ref.shape[0] - 1
    pooling = []
    for i, ref in enumerate((vol0_ref, vol1_ref, vol2_ref, vol3_ref)):
        nxt = 2 * ((i + 1) % 4)
        turning = turn_pieces(of(ref), jnp.minimum(4 * group + i + 3, top))
        total = first_dots((i + 1) % 2, mix(pooling, turning))
        total = second_dots(
            [2 * ((i + 3) % 4) + 1, 2 * i, 2 * i + 1, nxt], i == 3,
            first_pieces(total, [2, 2], [nxt, nxt + 1]), row_pieces(i % 2, [2, 2]),
        )
        pooling = second_pieces(i, total)
    for piece in pooling:
        piece()

    def leave(part, j):
        at = pl.multiple_of(part * 128, 128)
        return pltpu.make_async_copy(
            staged.at[part, j], sent_ref.at[jnp.maximum(slots[j], 0), :, pl.ds(at, 128)],
            sems.at[j],
        )

    for j in range(columns // 2):
        block = pooled[:, 32 * j:32 * j + 32, :].reshape(128, 128).T.astype(jnp.bfloat16)
        staged[group, j] = block[0:chans]
        staged[group, j + columns // 2] = block[chans:]
    for j in range(columns):
        @pl.when(slots[j] >= 0)
        def _():
            leave(group, j).start()

    @pl.when(last)
    def _():
        for j in range(columns):
            @pl.when(slots[j] >= 0)
            def _():
                for part in range(4):
                    leave(part, j).wait()


def local_features(order, near, far, volume, below, above, left, right, w1, b1, w2, b2):
    layers, chans, lanes = volume.shape
    columns = lanes // 128
    runs = lanes // (4 * SEG)
    pairs = layers // 2
    groups = 4 * near.shape[0]

    def whole(array):
        return pl.BlockSpec(array.shape, lambda g: (0,) * array.ndim)

    def pair(i):
        return pl.BlockSpec(
            (2, chans, lanes), lambda g: (jnp.minimum(4 * g + i + 2, pairs - 1), 0, 0)
        )

    scalar = pl.BlockSpec(memory_space=pltpu.SMEM)
    rows = runs * SEG
    return pl.pallas_call(
        features_kernel,
        grid=(pairs // 4,),
        in_specs=[
            scalar, scalar, scalar, scalar, scalar,
            pl.BlockSpec((4, chans, lanes), lambda g: (0, 0, 0)),
            pair(0), pair(1), pair(2), pair(3),
            whole(below), whole(above), whole(left), whole(right),
            whole(w1), whole(b1), whole(w2), whole(b2),
        ],
        out_specs=[pl.BlockSpec(memory_space=pl.ANY), scalar],
        out_shape=[
            jax.ShapeDtypeStruct((2 * groups, chans, 512), jnp.bfloat16),
            jax.ShapeDtypeStruct((columns // 2,), jnp.int32),
        ],
        scratch_shapes=[
            pltpu.VMEM((FRONT + SEG * (4 * runs + PAD) + 8, 128), jnp.float32),
            pltpu.VMEM((2, 2, rows + 4 * SEG, 256), jnp.bfloat16),
            pltpu.VMEM((9, rows + 2 * SEG, 256), jnp.bfloat16),
            pltpu.VMEM((3, len(BREAKS) - 1, SEG, 128), jnp.bfloat16),
            pltpu.VMEM((4, lanes // 8, 128), jnp.float32),
            pltpu.VMEM((4, columns, chans, 128), jnp.bfloat16),
            pltpu.SMEM((columns,), jnp.int32),
            pltpu.SemaphoreType.DMA((columns,)),
        ],
        compiler_params=pltpu.CompilerParams(vmem_limit_bytes=48 << 20),
        cost_estimate=pl.CostEstimate(
            flops=33_000_000_000, bytes_accessed=16_000_000, transcendentals=0
        ),
    )(order, near, *far, volume, volume, volume, volume, volume, below, above, left, right,
      w1, b1, w2, b2)


def banded(weight, taps):
    chans = weight.shape[0]
    parts = weight.reshape(chans, taps, 3, chans).transpose(1, 2, 3, 0)
    blank = jnp.zeros_like(parts[:, 0])
    rows = [
        jnp.concatenate(
            [parts[:, x - to + 1] if 0 <= x - to + 1 < 3 else blank for to in range(4)], axis=2
        )
        for x in range(4)
    ]
    return jnp.concatenate(rows, axis=1)


def per_device(volume, occupancy, device_order, weight_one, bias_one, weight_two, bias_two):
    layers, chans, lanes = volume.shape
    columns = occupancy.shape[1]
    groups = lax.axis_size("xy")
    tissue_row = occupancy[0]

    def swap(value, k):
        return lax.ppermute(value, "xy", [(i, i ^ k) for i in range(groups)])

    near = jnp.concatenate([occupancy] + [swap(occupancy, k) for k in (1, 2, 3)], axis=0)

    full = jnp.repeat(tissue_row, lanes // columns)[None, None, :] > 0
    empty = jnp.asarray(EMPTY, volume.dtype)
    below = shift(jnp.where(full, volume[layers - 1:], empty), "gz", 1)
    above = shift(jnp.where(full, volume[:1], empty), "gz", -1)

    def edge(start, mark):
        def turned(rows):
            pairs = rows.reshape(-1, 2, chans, 8).transpose(0, 3, 1, 2)
            return pairs.reshape(-1, 8, 2 * chans)

        own = jnp.where(mark > 0, volume[:, :, start:start + 8], empty)
        ends = [below[:, :, start:start + 8], above[:, :, start:start + 8]]
        return jnp.concatenate([turned(jnp.concatenate(ends, axis=0)), turned(own)], axis=0)

    left = shift(edge(lanes - 8, tissue_row[columns - 1]), "xy", 1)
    right = shift(edge(0, tissue_row[0]), "xy", -1)
    far = [swap(near, 4 * k) for k in (1, 2, 3)]

    w1, w2 = banded(weight_one, 3), banded(weight_two, 9)
    b1, b2 = jnp.tile(bias_one, 4)[None], jnp.tile(bias_two, 4)[None]
    sent, arrival = local_features(
        device_order, near, far, volume, below, above, left, right, w1, b1, w2, b2
    )
    arrived = lax.all_to_all(sent, "xy", split_axis=0, concat_axis=0, tiled=True)
    return jnp.take(arrived, arrival, axis=0, mode="clip")


def solution(mesh):
    in_specs = (P("gz", None, "xy"), P("gz", "xy"), P("gz", None), P(), P(), P(), P())
    out_specs = P(("gz", "xy"), None, None)
    return jax.shard_map(
        per_device, mesh=mesh, in_specs=in_specs, out_specs=out_specs, check_vma=False
    )
```

```python
import functools

import jax
import jax.numpy as jnp
from jax import lax
from jax.experimental import pallas as pl
from jax.experimental.pallas import tpu as pltpu
from jax.sharding import PartitionSpec as P

SEG = 16
HALF = 64


def shift(value, axis, step):
    peers = lax.axis_size(axis)
    pairs = [(i, i + step) for i in range(peers) if 0 <= i + step < peers]
    return lax.ppermute(value, axis, pairs)


EMPTY = 100.0
BREAKS = (-2, 0, 8, 16, 24, 32, 40, 42)


def span(t):
    return max(i for i, start in enumerate(BREAKS) if start <= t)


FRONT, PAD = 16, 4


class Spread:
    def __init__(self, work, steps):
        self.work, self.steps, self.done = list(work), steps, 0

    def step(self):
        self.done += 1
        for piece in self.work[
            len(self.work) * (self.done - 1) // self.steps:len(self.work) * self.done // self.steps
        ]:
            piece()


def mix(one, two):
    places = [((i + 0.5) / len(part), piece) for part in (one, two) for i, piece in enumerate(part)]
    return [piece for _, piece in sorted(places, key=lambda entry: entry[0])]


def counted(marks):
    counts = []
    for ref in marks:
        for row in range(ref.shape[0]):
            count = ref[row, 0]
            for j in range(1, ref.shape[1]):
                count = count + ref[row, j]
            counts.append(count)
    return counts


def arrival_kernel(order_ref, near_ref, far1_ref, far2_ref, far3_ref, arrival_ref):
    own = lax.axis_index("xy")
    counts = counted((near_ref, far1_ref, far2_ref, far3_ref))
    groups = len(counts)
    label = jnp.int32(0)
    for i in range(groups):
        label = label + jnp.where(order_ref[0, i] == own, i, 0)
    for k in range(groups):
        begin = jnp.int32(0)
        for m in range(groups):
            if m != k:
                begin = begin + jnp.where((own ^ m) < (own ^ k), counts[m], 0)
        for second in range(2):
            at = ((label - begin) & (groups - 1)) + groups * second

            @pl.when(at < counts[k])
            def _():
                arrival_ref[(begin + at) // groups] = 2 * (own ^ k) + second


def arrivals(order, near, far):
    scalar = pl.BlockSpec(memory_space=pltpu.SMEM)
    return pl.pallas_call(
        arrival_kernel,
        in_specs=[scalar] * 5,
        out_specs=scalar,
        out_shape=jax.ShapeDtypeStruct((near.shape[1] // 2,), jnp.int32),
    )(order, near, *far)


def banded(raw_ref, big_ref):
    chans = raw_ref.shape[0]
    turned = raw_ref[...].astype(jnp.float32).T
    blank = jnp.zeros((chans, chans), jnp.float32)
    for t in range(big_ref.shape[0]):
        strip = turned[3 * chans * t:3 * chans * (t + 1)]
        parts = [
            jnp.concatenate([strip[chans:], blank, blank], axis=0),
            jnp.concatenate([strip, blank], axis=0),
            jnp.concatenate([blank, strip], axis=0),
            jnp.concatenate([blank, blank, strip[:2 * chans]], axis=0),
        ]
        for h in range(2):
            both = jnp.concatenate(parts[2 * h:2 * h + 2], axis=1)
            big_ref[t, :, 128 * h:128 * h + 128] = both.astype(jnp.bfloat16)


def features_kernel(
    order_ref, near_ref, far1_ref, far2_ref, far3_ref, first_ref, vol0_ref, vol1_ref, vol2_ref, vol3_ref, below_ref, above_ref,
    left_ref, right_ref, raw1_ref, b1_ref, raw2_ref, b2_ref,
    sent_ref, w1_ref, w2_ref, flip, taps, hidden, masks, pooled, staged, slots, sems,
):
    group = pl.program_id(0)
    last = group == pl.num_programs(0) - 1
    chans, lanes = vol0_ref.shape[1], vol0_ref.shape[2]
    columns = lanes // 128
    runs = lanes // (4 * SEG)
    low = lax.broadcasted_iota(jnp.int32, (SEG, 128), 1) < HALF
    low8 = lax.broadcasted_iota(jnp.int32, (8, 128), 1) < HALF
    body_rows = runs * SEG
    first_rows = body_rows + 2 * SEG

    own = lax.axis_index("xy")
    groups = 4 * near_ref.shape[0]

    def route():
        counts = counted((near_ref, far1_ref, far2_ref, far3_ref))
        start = jnp.int32(0)
        for k in range(1, groups):
            start = start + jnp.where((own ^ k) < own, counts[k], 0)
        for j in range(columns):
            full = near_ref[0, j]
            to = order_ref[0, start & (groups - 1)]
            begin = start if j == 0 else begin
            second = (start - begin >= groups).astype(jnp.int32)
            slots[j] = jnp.where(full > 0, 2 * to + second, -1)
            start = start + full

    def turn_pieces(source, at_rim):
        def piece(j):
            block = jnp.concatenate([source(0, 128 * j), source(1, 128 * j)], axis=0)
            block = block.astype(jnp.float32).T
            start = 128 * j
            while start < 128 * j + 128:
                s = start // (4 * runs)
                stop = min(128 * j + 128, 4 * runs * (s + 1))
                to = FRONT + PAD * s + start
                flip[to:to + stop - start, :] = block[start - 128 * j:stop - 128 * j]
                start = stop

        def sides():
            flip[FRONT - PAD - 8:FRONT - PAD, :] = left_ref[at_rim].astype(jnp.float32)
            end = FRONT + SEG * (4 * runs + PAD)
            flip[end:end + 8, :] = right_ref[at_rim].astype(jnp.float32)

        return [sides] + [functools.partial(piece, j) for j in range(columns)]

    def turn(source, at_rim):
        for piece in turn_pieces(source, at_rim):
            piece()

    def row_tiles(t):
        start = FRONT + 4 * t + (-PAD if t < 0 else PAD if t >= runs else 0)
        rows = [flip[pl.ds(start + x, SEG, stride=4 * runs + PAD), :] for x in range(4)]
        turned = [pltpu.roll(row, HALF, 1) for row in rows]
        return [
            [
                jnp.where(low, rows[2 * h], turned[2 * h + 1]).astype(jnp.bfloat16)
                for h in range(2)
            ],
            [
                jnp.where(low, turned[2 * h], rows[2 * h + 1]).astype(jnp.bfloat16)
                for h in range(2)
            ],
        ]

    def store_taps(slot, layer, t, tiles, keep):
        for h in range(2):
            taps[slot, layer, SEG * (t + 2):SEG * (t + 3), 128 * h:128 * h + 128] = (
                tiles[layer][h] * keep
            )

    def row_pieces(slot, kinds):
        def piece(t):
            tiles = row_tiles(t)
            for layer in range(2):
                store_taps(slot, layer, t, tiles, masks[kinds[layer], span(t)])

        return [functools.partial(piece, t) for t in range(-2, runs + 2)]

    def first_dots(slot, work=()):
        total = None
        work = Spread(work, 3)
        for b in range(3):
            part = jnp.dot(
                taps[slot, :, SEG * b:SEG * b + first_rows, :].reshape(2 * first_rows, 256),
                w1_ref[b], preferred_element_type=jnp.float32,
            )
            total = part if total is None else total + part
            work.step()
        return total

    def first_pieces(total, kinds, places):
        def piece(layer, lo, hi, keep):
            at = layer * first_rows
            act = total[at + SEG * lo:at + SEG * hi]
            act = jnp.maximum(act + b1_ref[...], 0.0).astype(jnp.bfloat16)
            act = act.reshape(hi - lo, SEG, 256)
            for h in range(2):
                hidden[places[layer], SEG * lo:SEG * hi, 128 * h:128 * h + 128] = (
                    act[:, :, 128 * h:128 * h + 128] * keep()[None]
                ).reshape(SEG * (hi - lo), 128)

        made = []
        for layer in range(2):
            for i in range(len(BREAKS) - 1):
                lo, hi = max(BREAKS[i], -1) + 1, min(BREAKS[i + 1], runs + 1) + 1
                keep = functools.partial(lambda kind, i: masks[kind, i], kinds[layer], i)
                made.append(functools.partial(piece, layer, lo, hi, keep))
        return made

    def first_conv(slot, kinds, places):
        for piece in first_pieces(first_dots(slot), kinds, places):
            piece()

    def second_dots(places, ends, early, late):
        total = None
        early, late = Spread(early, 6), Spread(late, 9)
        for a in range(3):
            for b in range(3):
                rows = slice(SEG * b, SEG * b + body_rows)
                later = hidden[places[a + 1], rows, :]
                if ends and a == 2:
                    later = jnp.where(last, hidden[8, rows, :], later)
                part = jnp.dot(
                    jnp.concatenate([hidden[places[a], rows, :], later], axis=0),
                    w2_ref[3 * a + b], preferred_element_type=jnp.float32,
                )
                total = part if total is None else total + part
                if a < 2:
                    early.step()
                late.step()
        return total

    def second_pieces(slot, total):
        def piece(u):
            summed = None
            for at in (2 * u, 2 * u + 1, runs + 2 * u, runs + 2 * u + 1):
                part = jnp.maximum(total[SEG * at:SEG * at + SEG] + b2_ref[...], 0.0)
                summed = part if summed is None else summed + part
            for x2 in range(2):
                half = summed[:, 128 * x2:128 * x2 + 128]
                half = (half + pltpu.roll(half, HALF, 1)) * 0.125
                both = jnp.where(low8, half[0:8], half[8:16])
                pooled[slot, pl.ds(2 * u + x2, 8, stride=runs), :] = both

        return [functools.partial(piece, u) for u in range(runs // 2)]

    def of(ref):
        return lambda layer, at: ref[layer, :, at:at + 128]

    @pl.when(group == 0)
    def _():
        row = lax.broadcasted_iota(jnp.int32, (SEG, 128), 0)
        one, zero = jnp.ones((SEG, 128), jnp.bfloat16), jnp.zeros((SEG, 128), jnp.bfloat16)
        has = [
            lax.axis_index("gz") > 0, lax.axis_index("gz") < lax.axis_size("gz") - 1,
            own > 0, own < groups - 1,
        ]
        route()
        banded(raw1_ref, w1_ref)
        banded(raw2_ref, w2_ref)

        def inside(i):
            keep = None
            if BREAKS[i] < 0:
                keep = has[2] | (row > 0)
            elif BREAKS[i] >= runs:
                keep = has[3] | (row < SEG - 1)
            return keep

        turn(lambda layer, at: (below_ref, above_ref)[layer][0, :, at:at + 128], 0)
        for t in range(-2, runs + 2):
            tiles = row_tiles(t)
            for layer in range(2):
                i = span(t)
                if t == BREAKS[i]:
                    keep = (tiles[layer][0].astype(jnp.float32) < 50.0) & has[layer]
                    if inside(i) is not None:
                        keep = keep & inside(i)
                    masks[layer, i] = jnp.where(keep, 1.0, 0.0).astype(jnp.bfloat16)
                store_taps(0, layer, t, tiles, masks[layer, i])
        first_conv(0, [0, 1], [7, 8])

        turn(of(first_ref), 1)
        for i in range(len(BREAKS) - 1):
            t = BREAKS[i]
            keep = jnp.zeros((SEG, 128), jnp.float32)
            for s in range(SEG):
                column = (runs * s + t) // 32
                if 0 <= column < columns:
                    keep = jnp.where(row == s, near_ref[0, column].astype(jnp.float32), keep)
            keep = keep > 0.5
            seen = row_tiles(t)[0][0].astype(jnp.float32) < 50.0
            if t < 0:
                keep = keep | ((row == 0) & seen & has[2])
            elif t >= runs:
                keep = keep | ((row == SEG - 1) & seen & has[3])
            masks[2, i] = jnp.where(keep, 1.0, 0.0).astype(jnp.bfloat16)
        for t in range(-2, runs + 2):
            tiles = row_tiles(t)
            for layer in range(2):
                store_taps(0, layer, t, tiles, masks[2, span(t)])
        first_conv(0, [2, 2], [0, 1])
        turn(lambda layer, at: first_ref[2 + layer, :, at:at + 128], 2)
        for piece in row_pieces(1, [2, 2]):
            piece()

    top = left_ref.shape[0] - 1
    pooling = []
    for i, ref in enumerate((vol0_ref, vol1_ref, vol2_ref, vol3_ref)):
        nxt = 2 * ((i + 1) % 4)
        turning = turn_pieces(of(ref), jnp.minimum(4 * group + i + 3, top))
        total = first_dots((i + 1) % 2, mix(pooling, turning))
        total = second_dots(
            [2 * ((i + 3) % 4) + 1, 2 * i, 2 * i + 1, nxt], i == 3,
            first_pieces(total, [2, 2], [nxt, nxt + 1]), row_pieces(i % 2, [2, 2]),
        )
        pooling = second_pieces(i, total)
    for piece in pooling:
        piece()

    def leave(part, j):
        at = pl.multiple_of(part * 128, 128)
        return pltpu.make_async_copy(
            staged.at[part, j], sent_ref.at[jnp.maximum(slots[j], 0), :, pl.ds(at, 128)],
            sems.at[j],
        )

    for j in range(columns // 2):
        block = pooled[:, 32 * j:32 * j + 32, :].reshape(128, 128).T.astype(jnp.bfloat16)
        staged[group, j] = block[0:chans]
        staged[group, j + columns // 2] = block[chans:]
    for j in range(columns):
        @pl.when(slots[j] >= 0)
        def _():
            leave(group, j).start()

    @pl.when(last)
    def _():
        for j in range(columns):
            @pl.when(slots[j] >= 0)
            def _():
                for part in range(4):
                    leave(part, j).wait()


def local_features(order, near, far, volume, below, above, left, right, w1, b1, w2, b2):
    layers, chans, lanes = volume.shape
    columns = lanes // 128
    runs = lanes // (4 * SEG)
    pairs = layers // 2
    groups = 4 * near.shape[0]

    def whole(array):
        return pl.BlockSpec(array.shape, lambda g: (0,) * array.ndim)

    def pair(i):
        return pl.BlockSpec(
            (2, chans, lanes), lambda g: (jnp.minimum(4 * g + i + 2, pairs - 1), 0, 0)
        )

    scalar = pl.BlockSpec(memory_space=pltpu.SMEM)
    rows = runs * SEG
    return pl.pallas_call(
        features_kernel,
        grid=(pairs // 4,),
        in_specs=[
            scalar, scalar, scalar, scalar, scalar,
            pl.BlockSpec((4, chans, lanes), lambda g: (0, 0, 0)),
            pair(0), pair(1), pair(2), pair(3),
            whole(below), whole(above), whole(left), whole(right),
            whole(w1), whole(b1), whole(w2), whole(b2),
        ],
        out_specs=pl.BlockSpec(memory_space=pl.ANY),
        out_shape=jax.ShapeDtypeStruct((2 * groups, chans, 512), jnp.bfloat16),
        scratch_shapes=[
            pltpu.VMEM((3, 256, 256), jnp.bfloat16),
            pltpu.VMEM((9, 256, 256), jnp.bfloat16),
            pltpu.VMEM((FRONT + SEG * (4 * runs + PAD) + 8, 128), jnp.float32),
            pltpu.VMEM((2, 2, rows + 4 * SEG, 256), jnp.bfloat16),
            pltpu.VMEM((9, rows + 2 * SEG, 256), jnp.bfloat16),
            pltpu.VMEM((3, len(BREAKS) - 1, SEG, 128), jnp.bfloat16),
            pltpu.VMEM((4, lanes // 8, 128), jnp.float32),
            pltpu.VMEM((4, columns, chans, 128), jnp.bfloat16),
            pltpu.SMEM((columns,), jnp.int32),
            pltpu.SemaphoreType.DMA((columns,)),
        ],
        compiler_params=pltpu.CompilerParams(vmem_limit_bytes=48 << 20),
        cost_estimate=pl.CostEstimate(
            flops=33_000_000_000, bytes_accessed=16_000_000, transcendentals=0
        ),
    )(order, near, *far, volume, volume, volume, volume, volume, below, above, left, right,
      w1, b1, w2, b2)


def per_device(volume, occupancy, device_order, weight_one, bias_one, weight_two, bias_two):
    layers, chans, lanes = volume.shape
    columns = occupancy.shape[1]
    groups = lax.axis_size("xy")
    tissue_row = occupancy[0]

    def swap(value, k):
        return lax.ppermute(value, "xy", [(i, i ^ k) for i in range(groups)])

    near = jnp.concatenate([occupancy] + [swap(occupancy, k) for k in (1, 2, 3)], axis=0)

    full = jnp.repeat(tissue_row, lanes // columns)[None, None, :] > 0
    empty = jnp.asarray(EMPTY, volume.dtype)
    below = shift(jnp.where(full, volume[layers - 1:], empty), "gz", 1)
    above = shift(jnp.where(full, volume[:1], empty), "gz", -1)

    def edge(start, mark):
        def turned(rows):
            pairs = rows.reshape(-1, 2, chans, 8).transpose(0, 3, 1, 2)
            return pairs.reshape(-1, 8, 2 * chans)

        own = jnp.where(mark > 0, volume[:, :, start:start + 8], empty)
        ends = [below[:, :, start:start + 8], above[:, :, start:start + 8]]
        return jnp.concatenate([turned(jnp.concatenate(ends, axis=0)), turned(own)], axis=0)

    left = shift(edge(lanes - 8, tissue_row[columns - 1]), "xy", 1)
    right = shift(edge(0, tissue_row[0]), "xy", -1)
    far = [swap(near, 4 * k) for k in (1, 2, 3)]

    b1, b2 = jnp.tile(bias_one, 4)[None], jnp.tile(bias_two, 4)[None]
    sent = local_features(
        device_order, near, far, volume, below, above, left, right, weight_one, b1, weight_two, b2
    )
    arrival = arrivals(device_order, near, far)
    arrived = lax.all_to_all(sent, "xy", split_axis=0, concat_axis=0, tiled=True)
    return jnp.take(arrived, arrival, axis=0, mode="clip")


def solution(mesh):
    in_specs = (P("gz", None, "xy"), P("gz", "xy"), P("gz", None), P(), P(), P(), P())
    out_specs = P(("gz", "xy"), None, None)
    return jax.shard_map(
        per_device, mesh=mesh, in_specs=in_specs, out_specs=out_specs, check_vma=False
    )
```

```python
import functools

import jax
import jax.numpy as jnp
from jax import lax
from jax.experimental import pallas as pl
from jax.experimental.pallas import tpu as pltpu
from jax.sharding import PartitionSpec as P

SEG = 16
HALF = 64


def shift(value, axis, step):
    peers = lax.axis_size(axis)
    pairs = [(i, i + step) for i in range(peers) if 0 <= i + step < peers]
    return lax.ppermute(value, axis, pairs)


EMPTY = 100.0
BREAKS = (-2, 0, 8, 16, 24, 32, 40, 42)


def span(t):
    return max(i for i, start in enumerate(BREAKS) if start <= t)


FRONT, PAD = 16, 4


class Spread:
    def __init__(self, work, steps):
        self.work, self.steps, self.done = list(work), steps, 0

    def step(self):
        self.done += 1
        for piece in self.work[
            len(self.work) * (self.done - 1) // self.steps:len(self.work) * self.done // self.steps
        ]:
            piece()


def mix(one, two):
    places = [((i + 0.5) / len(part), piece) for part in (one, two) for i, piece in enumerate(part)]
    return [piece for _, piece in sorted(places, key=lambda entry: entry[0])]


def counted(marks):
    counts = []
    for ref in marks:
        for row in range(ref.shape[0]):
            count = ref[row, 0]
            for j in range(1, ref.shape[1]):
                count = count + ref[row, j]
            counts.append(count)
    return counts


def arrival_kernel(order_ref, near_ref, far1_ref, far2_ref, far3_ref, arrival_ref):
    own = lax.axis_index("xy")
    counts = counted((near_ref, far1_ref, far2_ref, far3_ref))
    groups = len(counts)
    label = jnp.int32(0)
    for i in range(groups):
        label = label + jnp.where(order_ref[0, i] == own, i, 0)
    for k in range(groups):
        begin = jnp.int32(0)
        for m in range(groups):
            if m != k:
                begin = begin + jnp.where((own ^ m) < (own ^ k), counts[m], 0)
        for second in range(2):
            at = ((label - begin) & (groups - 1)) + groups * second

            @pl.when(at < counts[k])
            def _():
                arrival_ref[(begin + at) // groups] = 2 * (own ^ k) + second


def arrivals(order, near, far):
    scalar = pl.BlockSpec(memory_space=pltpu.SMEM)
    return pl.pallas_call(
        arrival_kernel,
        in_specs=[scalar] * 5,
        out_specs=scalar,
        out_shape=jax.ShapeDtypeStruct((near.shape[1] // 2,), jnp.int32),
    )(order, near, *far)


def banded(raw_ref, big_ref):
    chans = raw_ref.shape[0]
    turned = raw_ref[...].astype(jnp.float32).T
    blank = jnp.zeros((chans, chans), jnp.float32)
    for t in range(big_ref.shape[0]):
        strip = turned[3 * chans * t:3 * chans * (t + 1)]
        parts = [
            jnp.concatenate([strip[chans:], blank, blank], axis=0),
            jnp.concatenate([strip, blank], axis=0),
            jnp.concatenate([blank, strip], axis=0),
            jnp.concatenate([blank, blank, strip[:2 * chans]], axis=0),
        ]
        for h in range(2):
            both = jnp.concatenate(parts[2 * h:2 * h + 2], axis=1)
            big_ref[t, :, 128 * h:128 * h + 128] = both.astype(jnp.bfloat16)


def features_kernel(
    order_ref, near_ref, far1_ref, far2_ref, far3_ref, first_ref, vol0_ref, vol1_ref, vol2_ref, vol3_ref, below_ref, above_ref,
    left_ref, right_ref, raw1_ref, bias1_ref, raw2_ref, bias2_ref,
    sent_ref, b1_ref, b2_ref, w1_ref, w2_ref, flip, taps, hidden, masks, pooled, staged, slots, sems,
):
    group = pl.program_id(0)
    last = group == pl.num_programs(0) - 1
    chans, lanes = vol0_ref.shape[1], vol0_ref.shape[2]
    columns = lanes // 128
    runs = lanes // (4 * SEG)
    low = lax.broadcasted_iota(jnp.int32, (SEG, 128), 1) < HALF
    low8 = lax.broadcasted_iota(jnp.int32, (8, 128), 1) < HALF
    body_rows = runs * SEG
    first_rows = body_rows + 2 * SEG

    own = lax.axis_index("xy")
    groups = 4 * near_ref.shape[0]

    def route():
        counts = counted((near_ref, far1_ref, far2_ref, far3_ref))
        start = jnp.int32(0)
        for k in range(1, groups):
            start = start + jnp.where((own ^ k) < own, counts[k], 0)
        for j in range(columns):
            full = near_ref[0, j]
            to = order_ref[0, start & (groups - 1)]
            begin = start if j == 0 else begin
            second = (start - begin >= groups).astype(jnp.int32)
            slots[j] = jnp.where(full > 0, 2 * to + second, -1)
            start = start + full

    def turn_pieces(source, at_rim):
        def piece(j):
            block = jnp.concatenate([source(0, 128 * j), source(1, 128 * j)], axis=0)
            block = block.astype(jnp.float32).T
            start = 128 * j
            while start < 128 * j + 128:
                s = start // (4 * runs)
                stop = min(128 * j + 128, 4 * runs * (s + 1))
                to = FRONT + PAD * s + start
                flip[to:to + stop - start, :] = block[start - 128 * j:stop - 128 * j]
                start = stop

        def sides():
            flip[FRONT - PAD - 8:FRONT - PAD, :] = left_ref[at_rim].astype(jnp.float32)
            end = FRONT + SEG * (4 * runs + PAD)
            flip[end:end + 8, :] = right_ref[at_rim].astype(jnp.float32)

        return [sides] + [functools.partial(piece, j) for j in range(columns)]

    def turn(source, at_rim):
        for piece in turn_pieces(source, at_rim):
            piece()

    def row_tiles(t):
        start = FRONT + 4 * t + (-PAD if t < 0 else PAD if t >= runs else 0)
        rows = [flip[pl.ds(start + x, SEG, stride=4 * runs + PAD), :] for x in range(4)]
        turned = [pltpu.roll(row, HALF, 1) for row in rows]
        return [
            [
                jnp.where(low, rows[2 * h], turned[2 * h + 1]).astype(jnp.bfloat16)
                for h in range(2)
            ],
            [
                jnp.where(low, turned[2 * h], rows[2 * h + 1]).astype(jnp.bfloat16)
                for h in range(2)
            ],
        ]

    def store_taps(slot, layer, t, tiles, keep):
        for h in range(2):
            taps[slot, layer, SEG * (t + 2):SEG * (t + 3), 128 * h:128 * h + 128] = (
                tiles[layer][h] * keep
            )

    def row_pieces(slot, kinds):
        def piece(t):
            tiles = row_tiles(t)
            for layer in range(2):
                store_taps(slot, layer, t, tiles, masks[kinds[layer], span(t)])

        return [functools.partial(piece, t) for t in range(-2, runs + 2)]

    def first_dots(slot, work=()):
        total = None
        work = Spread(work, 3)
        for b in range(3):
            part = jnp.dot(
                taps[slot, :, SEG * b:SEG * b + first_rows, :].reshape(2 * first_rows, 256),
                w1_ref[b], preferred_element_type=jnp.float32,
            )
            total = part if total is None else total + part
            work.step()
        return total

    def first_pieces(total, kinds, places):
        def piece(layer, lo, hi, keep):
            at = layer * first_rows
            act = total[at + SEG * lo:at + SEG * hi]
            act = jnp.maximum(act + b1_ref[...], 0.0).astype(jnp.bfloat16)
            act = act.reshape(hi - lo, SEG, 256)
            for h in range(2):
                hidden[places[layer], SEG * lo:SEG * hi, 128 * h:128 * h + 128] = (
                    act[:, :, 128 * h:128 * h + 128] * keep()[None]
                ).reshape(SEG * (hi - lo), 128)

        made = []
        for layer in range(2):
            for i in range(len(BREAKS) - 1):
                lo, hi = max(BREAKS[i], -1) + 1, min(BREAKS[i + 1], runs + 1) + 1
                keep = functools.partial(lambda kind, i: masks[kind, i], kinds[layer], i)
                made.append(functools.partial(piece, layer, lo, hi, keep))
        return made

    def first_conv(slot, kinds, places):
        for piece in first_pieces(first_dots(slot), kinds, places):
            piece()

    def second_dots(places, ends, early, late):
        total = None
        early, late = Spread(early, 6), Spread(late, 9)
        for a in range(3):
            for b in range(3):
                rows = slice(SEG * b, SEG * b + body_rows)
                later = hidden[places[a + 1], rows, :]
                if ends and a == 2:
                    later = jnp.where(last, hidden[8, rows, :], later)
                part = jnp.dot(
                    jnp.concatenate([hidden[places[a], rows, :], later], axis=0),
                    w2_ref[3 * a + b], preferred_element_type=jnp.float32,
                )
                total = part if total is None else total + part
                if a < 2:
                    early.step()
                late.step()
        return total

    def second_pieces(slot, total):
        def piece(u):
            summed = None
            for at in (2 * u, 2 * u + 1, runs + 2 * u, runs + 2 * u + 1):
                part = jnp.maximum(total[SEG * at:SEG * at + SEG] + b2_ref[...], 0.0)
                summed = part if summed is None else summed + part
            for x2 in range(2):
                half = summed[:, 128 * x2:128 * x2 + 128]
                half = (half + pltpu.roll(half, HALF, 1)) * 0.125
                both = jnp.where(low8, half[0:8], half[8:16])
                pooled[slot, pl.ds(2 * u + x2, 8, stride=runs), :] = both

        return [functools.partial(piece, u) for u in range(runs // 2)]

    def of(ref):
        return lambda layer, at: ref[layer, :, at:at + 128]

    @pl.when(group == 0)
    def _():
        row = lax.broadcasted_iota(jnp.int32, (SEG, 128), 0)
        one, zero = jnp.ones((SEG, 128), jnp.bfloat16), jnp.zeros((SEG, 128), jnp.bfloat16)
        has = [
            lax.axis_index("gz") > 0, lax.axis_index("gz") < lax.axis_size("gz") - 1,
            own > 0, own < groups - 1,
        ]
        route()
        for bias_ref, b_ref in ((bias1_ref, b1_ref), (bias2_ref, b2_ref)):
            b_ref[...] = jnp.concatenate([bias_ref[...]] * 4, axis=1)
        banded(raw1_ref, w1_ref)
        banded(raw2_ref, w2_ref)

        def inside(i):
            keep = None
            if BREAKS[i] < 0:
                keep = has[2] | (row > 0)
            elif BREAKS[i] >= runs:
                keep = has[3] | (row < SEG - 1)
            return keep

        turn(lambda layer, at: (below_ref, above_ref)[layer][0, :, at:at + 128], 0)
        for t in range(-2, runs + 2):
            tiles = row_tiles(t)
            for layer in range(2):
                i = span(t)
                if t == BREAKS[i]:
                    keep = (tiles[layer][0].astype(jnp.float32) < 50.0) & has[layer]
                    if inside(i) is not None:
                        keep = keep & inside(i)
                    masks[layer, i] = jnp.where(keep, 1.0, 0.0).astype(jnp.bfloat16)
                store_taps(0, layer, t, tiles, masks[layer, i])
        first_conv(0, [0, 1], [7, 8])

        turn(of(first_ref), 1)
        for i in range(len(BREAKS) - 1):
            t = BREAKS[i]
            keep = jnp.zeros((SEG, 128), jnp.float32)
            for s in range(SEG):
                column = (runs * s + t) // 32
                if 0 <= column < columns:
                    keep = jnp.where(row == s, near_ref[0, column].astype(jnp.float32), keep)
            keep = keep > 0.5
            seen = row_tiles(t)[0][0].astype(jnp.float32) < 50.0
            if t < 0:
                keep = keep | ((row == 0) & seen & has[2])
            elif t >= runs:
                keep = keep | ((row == SEG - 1) & seen & has[3])
            masks[2, i] = jnp.where(keep, 1.0, 0.0).astype(jnp.bfloat16)
        for t in range(-2, runs + 2):
            tiles = row_tiles(t)
            for layer in range(2):
                store_taps(0, layer, t, tiles, masks[2, span(t)])
        first_conv(0, [2, 2], [0, 1])
        turn(lambda layer, at: first_ref[2 + layer, :, at:at + 128], 2)
        for piece in row_pieces(1, [2, 2]):
            piece()

    top = left_ref.shape[0] - 1
    pooling = []
    for i, ref in enumerate((vol0_ref, vol1_ref, vol2_ref, vol3_ref)):
        nxt = 2 * ((i + 1) % 4)
        turning = turn_pieces(of(ref), jnp.minimum(4 * group + i + 3, top))
        total = first_dots((i + 1) % 2, mix(pooling, turning))
        total = second_dots(
            [2 * ((i + 3) % 4) + 1, 2 * i, 2 * i + 1, nxt], i == 3,
            first_pieces(total, [2, 2], [nxt, nxt + 1]), row_pieces(i % 2, [2, 2]),
        )
        pooling = second_pieces(i, total)
    for piece in pooling:
        piece()

    def leave(part, j):
        at = pl.multiple_of(part * 128, 128)
        return pltpu.make_async_copy(
            staged.at[part, j], sent_ref.at[jnp.maximum(slots[j], 0), :, pl.ds(at, 128)],
            sems.at[j],
        )

    for j in range(columns // 2):
        block = pooled[:, 32 * j:32 * j + 32, :].reshape(128, 128).T.astype(jnp.bfloat16)
        staged[group, j] = block[0:chans]
        staged[group, j + columns // 2] = block[chans:]
    for j in range(columns):
        @pl.when(slots[j] >= 0)
        def _():
            leave(group, j).start()

    @pl.when(last)
    def _():
        for j in range(columns):
            @pl.when(slots[j] >= 0)
            def _():
                for part in range(4):
                    leave(part, j).wait()


def local_features(order, near, far, volume, below, above, left, right, w1, b1, w2, b2):
    layers, chans, lanes = volume.shape
    columns = lanes // 128
    runs = lanes // (4 * SEG)
    pairs = layers // 2
    groups = 4 * near.shape[0]

    def whole(array):
        return pl.BlockSpec(array.shape, lambda g: (0,) * array.ndim)

    def pair(i):
        return pl.BlockSpec(
            (2, chans, lanes), lambda g: (jnp.minimum(4 * g + i + 2, pairs - 1), 0, 0)
        )

    scalar = pl.BlockSpec(memory_space=pltpu.SMEM)
    rows = runs * SEG
    return pl.pallas_call(
        features_kernel,
        grid=(pairs // 4,),
        in_specs=[
            scalar, scalar, scalar, scalar, scalar,
            pl.BlockSpec((4, chans, lanes), lambda g: (0, 0, 0)),
            pair(0), pair(1), pair(2), pair(3),
            whole(below), whole(above), whole(left), whole(right),
            whole(w1), whole(b1), whole(w2), whole(b2),
        ],
        out_specs=pl.BlockSpec(memory_space=pl.ANY),
        out_shape=jax.ShapeDtypeStruct((2 * groups, chans, 512), jnp.bfloat16),
        scratch_shapes=[
            pltpu.VMEM((1, 4 * chans), jnp.float32),
            pltpu.VMEM((1, 4 * chans), jnp.float32),
            pltpu.VMEM((3, 256, 256), jnp.bfloat16),
            pltpu.VMEM((9, 256, 256), jnp.bfloat16),
            pltpu.VMEM((FRONT + SEG * (4 * runs + PAD) + 8, 128), jnp.float32),
            pltpu.VMEM((2, 2, rows + 4 * SEG, 256), jnp.bfloat16),
            pltpu.VMEM((9, rows + 2 * SEG, 256), jnp.bfloat16),
            pltpu.VMEM((3, len(BREAKS) - 1, SEG, 128), jnp.bfloat16),
            pltpu.VMEM((4, lanes // 8, 128), jnp.float32),
            pltpu.VMEM((4, columns, chans, 128), jnp.bfloat16),
            pltpu.SMEM((columns,), jnp.int32),
            pltpu.SemaphoreType.DMA((columns,)),
        ],
        compiler_params=pltpu.CompilerParams(vmem_limit_bytes=62 << 20),
        cost_estimate=pl.CostEstimate(
            flops=33_000_000_000, bytes_accessed=16_000_000, transcendentals=0
        ),
    )(order, near, *far, volume, volume, volume, volume, volume, below, above, left, right,
      w1, b1, w2, b2)


def per_device(volume, occupancy, device_order, weight_one, bias_one, weight_two, bias_two):
    layers, chans, lanes = volume.shape
    columns = occupancy.shape[1]
    groups = lax.axis_size("xy")
    tissue_row = occupancy[0]

    def swap(value, k):
        return lax.ppermute(value, "xy", [(i, i ^ k) for i in range(groups)])

    near = jnp.concatenate([occupancy] + [swap(occupancy, k) for k in (1, 2, 3)], axis=0)

    full = jnp.repeat(tissue_row, lanes // columns)[None, None, :] > 0
    empty = jnp.asarray(EMPTY, volume.dtype)
    below = shift(jnp.where(full, volume[layers - 1:], empty), "gz", 1)
    above = shift(jnp.where(full, volume[:1], empty), "gz", -1)

    def edge(start, mark):
        def turned(rows):
            pairs = rows.reshape(-1, 2, chans, 8).transpose(0, 3, 1, 2)
            return pairs.reshape(-1, 8, 2 * chans)

        own = jnp.where(mark > 0, volume[:, :, start:start + 8], empty)
        ends = [below[:, :, start:start + 8], above[:, :, start:start + 8]]
        return jnp.concatenate([turned(jnp.concatenate(ends, axis=0)), turned(own)], axis=0)

    left = shift(edge(lanes - 8, tissue_row[columns - 1]), "xy", 1)
    right = shift(edge(0, tissue_row[0]), "xy", -1)
    far = [swap(near, 4 * k) for k in (1, 2, 3)]

    b1, b2 = bias_one[None], bias_two[None]
    sent = local_features(
        device_order, near, far, volume, below, above, left, right, weight_one, b1, weight_two, b2
    )
    arrival = arrivals(device_order, near, far)
    arrived = lax.all_to_all(sent, "xy", split_axis=0, concat_axis=0, tiled=True)
    return jnp.take(arrived, arrival, axis=0, mode="clip")


def solution(mesh):
    in_specs = (P("gz", None, "xy"), P("gz", "xy"), P("gz", None), P(), P(), P(), P())
    out_specs = P(("gz", "xy"), None, None)
    return jax.shard_map(
        per_device, mesh=mesh, in_specs=in_specs, out_specs=out_specs, check_vma=False
    )
```
